256 devices in a mesh: expert: 64 (over z, y, core), dp: 4 (over x).
Axes of the slice: x: 4, y: 4, z: 8, core: 2. Of those that a mesh axis runs over, the one named last changes fastest.
Arguments:
- prenorm_input: bfloat16 [32768, 1280], P(('expert', 'dp')), may hold values from -6 to 6
- gain: float32 [1280], replicated, may hold values from 0.25 to 1.75
- router: bfloat16 [1280, 32], replicated, may hold values from -0.15625 to 0.15625
- routes: int32 [32768, 2], P(('expert', 'dp')), may hold values from 0 to 31, all different within a row; in each aligned block of 128 rows (0 to 127, 128 to 255, ...) at most 10 rows name the same one
- w_in: bfloat16 [64, 1280, 1280], P('expert', None, 'dp'), may hold values from -0.15625 to 0.15625
- w_out: bfloat16 [64, 1280, 1280], P('expert', 'dp'), may hold values from -0.125 to 0.125
- cotangent: bfloat16 [32768, 1280], P(('expert', 'dp')), may hold values from -18 to 18
Outputs:
- input_grad: bfloat16 [32768, 1280], P(('expert', 'dp'))
- grad_in: bfloat16 [64, 1280, 1280], P('expert', None, 'dp')
- grad_out: bfloat16 [64, 1280, 1280], P('expert', 'dp')
- grad_router: float32 [1280, 32], replicated
- grad_gain: float32 [1280], replicated
The draws below stay inside these ranges and needn't reach their ends.
Inputs may be any that keep to these rules, and one draw needn't show every extreme that they name: `routes`: each row names 2 different experts; among the rows of one device no expert is named more than 10 times.
All inputs are finite; a program needn't handle non-finite values.
Results may differ from the reference program's by a relative error of at most 0.015.
Values may be sent and summed in bfloat16 or wider, within the bound.
A program may use at most 128 MiB of HBM per device.

```python
import math
import jax
import jax.numpy as jnp
import numpy as np
from jax import lax

MODEL_WIDTH = 1280
FF = 2560
CHOSEN_EXPERTS = 2
DEVICE_TOKENS = 128
EXPERTS = 32
CAP = 10
TOKENS = 32768


def draw_cotangent(key, part):
    key_base, key_rows, key_cols = jax.random.split(key, 3)
    positions = jnp.arange(TOKENS).astype(jnp.float32)
    ramp = 0.5 + positions / TOKENS
    row_scale = ramp * jnp.exp(jax.random.uniform(key_rows, (TOKENS,), jnp.float32, 0.0, math.log(4.0)))
    col_scale = jnp.exp(jax.random.uniform(key_cols, (MODEL_WIDTH,), jnp.float32, 0.0, math.log(3.0)))
    base = jnp.clip(jax.random.normal(key_base, (TOKENS, MODEL_WIDTH), jnp.float32), -4.0, 4.0)
    return (0.25 * base * row_scale[:, None] * col_scale[None, :]).astype(jnp.bfloat16)


def steps_of(stream_key, shape, cuts, smallest, top_value):
    def one(position, blocks):
        draws = jax.random.uniform(jax.random.fold_in(jax.random.fold_in(stream_key, 6), position), (blocks,), jnp.float32, smallest / len(cuts), top_value / len(cuts))
        return jnp.repeat(jnp.exp(draws), shape[position] // blocks).reshape((-1,) + (1,) * (len(shape) - position - 1))

    level = one(*cuts[0])
    for cut in cuts[1:]:
        level = level * one(*cut)
    return level


def shared_out(stream_key, own, number, rows, number_of, top, bound, lean):
    sequence = jax.random.permutation(stream_key, number_of)
    crowded, usual = portions_of(number_of, rows * top, bound, lean, True), portions_of(number_of, rows * top, bound, lean, False)
    places = jnp.arange(number_of)

    def named(sizes, rotation):
        used = int((sizes > 0).sum())
        fixed = max(1, used // 4)
        passed = fixed + (places - fixed + rotation * (used - fixed)) % max(1, number_of - fixed)
        return jnp.zeros((number_of,), jnp.int32).at[sequence[jnp.where(places < fixed, places, passed)]].set(jnp.asarray(sizes, jnp.int32))

    sizes = jnp.where(number % 4 == 0, named(crowded, number // 4), named(usual, number - number // 4 - 1))
    mixed = jax.random.permutation(jax.random.fold_in(own, 3), number_of)
    giver, sink = mixed[0:number_of // 2 * 2:2], mixed[1:number_of // 2 * 2:2]
    slack = jnp.minimum(sizes[giver] - 1, bound - sizes[sink]) // 2
    slack = jnp.where((giver == sequence[0]) | (sink == sequence[0]) | (sizes[sink] == 0), 0, jnp.maximum(slack, 0))
    passed = jax.random.randint(jax.random.fold_in(own, 4), (number_of // 2,), 0, 1 << 20) % (slack + 1)
    sizes = sizes.at[giver].add(-passed).at[sink].add(passed)
    members = jnp.searchsorted(jnp.cumsum(sizes), jnp.arange(rows * top), side="right").astype(jnp.int32)
    table = members.reshape(top, rows).T
    table = table[jax.random.permutation(jax.random.fold_in(own, 1), rows)]
    rotation = jax.random.randint(jax.random.fold_in(own, 2), (rows, 1), 0, top)
    return jnp.take_along_axis(table, (jnp.arange(top)[None, :] + rotation) % top, axis=1)


def portions_of(count, total, most, skew, full):
    portions = [(1 << 20) // math.isqrt(rank ** skew) + 1 for rank in range(1, count + 1)]
    largest = most if full else min(most, max(-(-total // count), total * portions[0] // sum(portions)))
    least = 1 if total - largest >= count - 1 else 0
    given, surplus = [largest] + [least] * (count - 1), total - largest - least * (count - 1)
    while surplus > 0:
        free = [i for i in range(1, count) if given[i] < largest] or [i for i in range(1, count) if given[i] < most]
        mass, left = sum([portions[i] for i in free]), surplus
        for i in free:
            more = min(most - given[i], max(1, left * portions[i] // mass), surplus)
            given[i] = given[i] + more
            surplus = surplus - more
    return np.array(given)


def bell_draw(key, extent, spread, most, cuts=(), kind=jnp.bfloat16):
    values = spread * jax.random.normal(key, extent, jnp.float32)
    if cuts:
        values = values * steps_of(key, extent, cuts, -0.22, 0.18)
    return jnp.clip(values, -most, most).astype(kind)


def setup_inputs(seed: int = 0) -> dict:
    seeds = jax.random.split(jax.random.key(seed), 8)
    prenorm_input = bell_draw(seeds[0], (TOKENS, MODEL_WIDTH), 1.0, 6.0, ((0, 256),))
    gain = jnp.clip(1.0 + 0.15 * jax.random.normal(seeds[1], (MODEL_WIDTH,), jnp.float32), 0.25, 1.75)
    router = bell_draw(seeds[2], (MODEL_WIDTH, EXPERTS), MODEL_WIDTH ** -0.5, 0.15625)
    routes_keys = jax.random.split(jax.random.fold_in(seeds[3], 1), TOKENS // DEVICE_TOKENS)
    routes_turns = jax.random.permutation(jax.random.fold_in(seeds[3], 3), TOKENS // DEVICE_TOKENS)
    routes = jax.vmap(lambda own, number: shared_out(jax.random.fold_in(seeds[3], 2), own, number, DEVICE_TOKENS, EXPERTS, CHOSEN_EXPERTS, CAP, 2))(routes_keys, routes_turns).reshape((TOKENS, CHOSEN_EXPERTS))
    w_in = bell_draw(seeds[4], (2 * EXPERTS, MODEL_WIDTH, FF // 2), MODEL_WIDTH ** -0.5, 0.15625, ((0, 64), (2, 4)))
    w_out = bell_draw(seeds[5], (2 * EXPERTS, FF // 2, MODEL_WIDTH), FF ** -0.5, 0.125, ((0, 64), (1, 4)))
    cotangent = draw_cotangent(jax.random.fold_in(seeds[7], 71), 0)
    return dict(prenorm_input=prenorm_input, gain=gain, router=router, routes=routes, w_in=w_in, w_out=w_out, cotangent=cotangent)


def gelu_parts(pre):
    coeff = math.sqrt(2.0 / math.pi)
    inner = coeff * (pre + 0.044715 * pre * pre * pre)
    tanh_val = jnp.tanh(inner)
    value = 0.5 * pre * (1.0 + tanh_val)
    slope = 0.5 * (1.0 + tanh_val) + 0.5 * pre * (1.0 - tanh_val * tanh_val) * coeff * (1.0 + 3.0 * 0.044715 * pre * pre)
    return (value, slope)

def norm_pieces(block, gain):
    values = block.astype(jnp.float32)
    centred_rows = values - lax.optimization_barrier(jnp.mean(values, axis=1, keepdims=True))
    inverse_deviation = lax.rsqrt(lax.optimization_barrier(jnp.mean(centred_rows * centred_rows, axis=1, keepdims=True)) + 1e-06)
    normalized_rows = centred_rows * inverse_deviation
    return (normalized_rows, inverse_deviation, (normalized_rows * gain[None, :]).astype(jnp.bfloat16))

def slot_index(routing_rows, expert_list, expert_capacity):
    flat = routing_rows.reshape(-1).astype(jnp.int32)
    onehot = (flat[:, None] == jnp.arange(expert_list, dtype=jnp.int32)[None, :]).astype(jnp.int32)
    before = (jnp.cumsum(onehot, axis=0) - onehot).astype(jnp.int32)
    slot = lax.optimization_barrier(jnp.sum(before * onehot, axis=1)).astype(jnp.int32)
    return (flat * expert_capacity + slot).astype(jnp.int32)

def place_matrix(where, slots):
    return where[None, :] == jnp.arange(slots, dtype=jnp.int32)[:, None]

def expert_pass(rows_m, rows_d, column, w_first, w_second):
    gate = jax.nn.sigmoid(jnp.dot(rows_m, column, preferred_element_type=jnp.float32)[:, 0])
    pre = jnp.dot(rows_m, w_first, preferred_element_type=jnp.float32)
    value, slope = gelu_parts(pre)
    hidden = value.astype(jnp.bfloat16)
    back = jnp.dot(rows_d, w_second.T, preferred_element_type=jnp.float32)
    gate_gradient = lax.optimization_barrier(jnp.sum(hidden.astype(jnp.float32) * back, axis=1))
    grad_pre = (gate[:, None] * back * slope).astype(jnp.bfloat16)
    grad_y = (gate[:, None] * rows_d.astype(jnp.float32)).astype(jnp.bfloat16)
    grad_second = jnp.dot(hidden.T, grad_y, preferred_element_type=jnp.float32)
    grad_first = jnp.dot(rows_m.T, grad_pre, preferred_element_type=jnp.float32)
    row_gradient = jnp.dot(grad_pre, w_first.T, preferred_element_type=jnp.float32)
    return (row_gradient, gate_gradient, grad_first, grad_second)

def token_gradient(mixed_rows, normalized_rows, inverse_deviation, cotangent, routing_rows, gain, router, slot_gradient, slot_gate_gradient, expert_list, expert_capacity):
    where = slot_index(routing_rows, expert_list, expert_capacity)
    tok = mixed_rows.shape[0]
    top = routing_rows.shape[1]
    hi = lax.Precision.HIGHEST
    grad_assign = jnp.take(slot_gradient, where, axis=0)
    grad_expert = lax.optimization_barrier(jnp.sum(grad_assign.reshape(tok, top, -1), axis=1))
    gate_gradient = jnp.take(slot_gate_gradient, where, axis=0).reshape(tok, top)
    logits = jnp.dot(mixed_rows, router, preferred_element_type=jnp.float32)
    choose = (routing_rows[:, :, None] == jnp.arange(expert_list, dtype=jnp.int32)[None, None, :]).astype(jnp.float32)
    gates = jax.nn.sigmoid(lax.optimization_barrier(jnp.sum(choose * logits[:, None, :], axis=2)))
    dlogit = lax.optimization_barrier(jnp.sum(choose * (gate_gradient * gates * (1.0 - gates))[:, :, None], axis=1))
    mixed_gradient = grad_expert + jnp.dot(dlogit, router.astype(jnp.float32).T, precision=hi)
    router_term = jnp.dot(mixed_rows.astype(jnp.float32).T, dlogit, precision=hi)
    gain_product = lax.optimization_barrier(jnp.sum(mixed_gradient * normalized_rows, axis=0))
    scaled_rows = mixed_gradient * gain[None, :]
    mean_first_term = lax.optimization_barrier(jnp.mean(scaled_rows, axis=1, keepdims=True))
    mean_second_term = lax.optimization_barrier(jnp.mean(scaled_rows * normalized_rows, axis=1, keepdims=True))
    norm_backward = inverse_deviation * (scaled_rows - mean_first_term - normalized_rows * mean_second_term)
    final_result = (cotangent.astype(jnp.float32) + norm_backward).astype(jnp.bfloat16)
    return (final_result, router_term, gain_product)

def reference(prenorm_input, gain, router, routes, w_in, w_out, cotangent):
    block_list = TOKENS // DEVICE_TOKENS
    slots = EXPERTS * CAP
    half = FF // 2
    normalized_rows, inverse_deviation, mixed_rows = norm_pieces(prenorm_input, gain)
    full_in = w_in.reshape(EXPERTS, 2, MODEL_WIDTH, half).transpose(0, 2, 1, 3).reshape(EXPERTS, MODEL_WIDTH, FF)
    full_out = w_out.reshape(EXPERTS, FF, MODEL_WIDTH)

    def dispatch(items):
        m_blk, d_blk, r_blk = items
        places = place_matrix(slot_index(r_blk, EXPERTS, CAP), slots).astype(jnp.bfloat16)
        send_m = jnp.dot(places, jnp.repeat(m_blk, CHOSEN_EXPERTS, axis=0), preferred_element_type=jnp.float32).astype(jnp.bfloat16)
        send_d = jnp.dot(places, jnp.repeat(d_blk, CHOSEN_EXPERTS, axis=0), preferred_element_type=jnp.float32).astype(jnp.bfloat16)
        return (send_m, send_d)
    send_m, send_d = lax.map(dispatch, (mixed_rows.reshape(block_list, DEVICE_TOKENS, MODEL_WIDTH), cotangent.reshape(block_list, DEVICE_TOKENS, MODEL_WIDTH), routes.reshape(block_list, DEVICE_TOKENS, CHOSEN_EXPERTS)))

    def by_expert(stack):
        return stack.reshape(block_list, EXPERTS, CAP, MODEL_WIDTH).transpose(1, 0, 2, 3).reshape(EXPERTS, block_list * CAP, MODEL_WIDTH)
    columns = router.T[:, :, None]

    def per_expert(items):
        rows_m, rows_d, column, w_first, w_second = items
        return expert_pass(rows_m, rows_d, column, w_first, w_second)
    row_gradient, gate_gradient, grad_first, grad_second = lax.map(per_expert, (by_expert(send_m), by_expert(send_d), columns, full_in, full_out))
    row_gradient = row_gradient.reshape(EXPERTS, block_list, CAP, MODEL_WIDTH).transpose(1, 0, 2, 3).reshape(block_list, slots, MODEL_WIDTH)
    gate_gradient = gate_gradient.reshape(EXPERTS, block_list, CAP).transpose(1, 0, 2).reshape(block_list, slots)

    def combine_rows(items):
        m_blk, x_blk, s_blk, d_blk, r_blk, g_blk, q_blk = items
        return token_gradient(m_blk, x_blk, s_blk, d_blk, r_blk, gain, router, g_blk, q_blk, EXPERTS, CAP)
    final_result, router_pieces, gain_products = lax.map(combine_rows, (mixed_rows.reshape(block_list, DEVICE_TOKENS, MODEL_WIDTH), normalized_rows.reshape(block_list, DEVICE_TOKENS, MODEL_WIDTH), inverse_deviation.reshape(block_list, DEVICE_TOKENS, 1), cotangent.reshape(block_list, DEVICE_TOKENS, MODEL_WIDTH), routes.reshape(block_list, DEVICE_TOKENS, CHOSEN_EXPERTS), row_gradient, gate_gradient))
    grad_in = grad_first.astype(jnp.bfloat16).reshape(EXPERTS, MODEL_WIDTH, 2, half).transpose(0, 2, 1, 3).reshape(2 * EXPERTS, MODEL_WIDTH, half)
    grad_out = grad_second.astype(jnp.bfloat16).reshape(2 * EXPERTS, half, MODEL_WIDTH)
    return (final_result.reshape(TOKENS, MODEL_WIDTH), grad_in, grad_out, lax.optimization_barrier(jnp.sum(router_pieces, axis=0)), lax.optimization_barrier(jnp.sum(gain_products, axis=0)))
```

```python
import math

import jax
import jax.numpy as jnp
from jax import lax
from jax.sharding import PartitionSpec as P

F32 = jnp.float32
BF16 = jnp.bfloat16


def gelu_parts(pre):
    coeff = math.sqrt(2.0 / math.pi)
    inner = coeff * (pre + 0.044715 * pre * pre * pre)
    tanh_val = jnp.tanh(inner)
    value = 0.5 * pre * (1.0 + tanh_val)
    slope = 0.5 * (1.0 + tanh_val) + 0.5 * pre * (1.0 - tanh_val * tanh_val) * coeff * (
        1.0 + 3.0 * 0.044715 * pre * pre
    )
    return (value, slope)


def dot(a, b):
    return jnp.dot(a, b, preferred_element_type=F32)


def dot_nt(a, b):
    return lax.dot_general(a, b, (((1,), (1,)), ((), ())), preferred_element_type=F32)


def dot_tn(a, b):
    return lax.dot_general(a, b, (((0,), (0,)), ((), ())), preferred_element_type=F32)


def norm_pieces(block, gain):
    values = block.astype(F32)
    centred = values - jnp.mean(values, axis=1, keepdims=True)
    inv = lax.rsqrt(jnp.mean(centred * centred, axis=1, keepdims=True) + 1e-06)
    xhat = centred * inv
    return xhat, inv, (xhat * gain[None, :]).astype(BF16)


def slot_ids(routes, experts):
    tok = routes.shape[0]
    eye = jnp.arange(experts, dtype=jnp.int32)
    hot = (routes[:, :, None] == eye).astype(F32)
    named = jnp.sum(hot, axis=1).astype(BF16)
    lower = (jnp.arange(tok)[:, None] > jnp.arange(tok)[None, :]).astype(BF16)
    before = dot(lower, named)
    slot = jnp.sum(before[:, None, :] * hot, axis=2).astype(jnp.int32)
    return routes * 16 + slot


def pack_messages(ids, mixed, cot, experts):
    width = mixed.shape[1]
    half = width // 2
    row = jnp.arange(experts * 8, dtype=jnp.int32)
    main = (row // 8) * 16 + row % 8
    rest = (row // 8) * 16 + 8 + row % 2
    part = (row % 8) // 2
    first, second = ids[:, 0][None, :], ids[:, 1][None, :]
    place = ((main[:, None] == first) | (main[:, None] == second)).astype(BF16)
    late = (rest[:, None] == first) | (rest[:, None] == second)
    late = jnp.concatenate([late & (part == i)[:, None] for i in range(4)], axis=1).astype(BF16)
    source = jnp.concatenate([mixed[:, :half], cot[:, :half], mixed[:, half:], cot[:, half:]], axis=0)
    out = jnp.concatenate([dot(place, mixed), dot(place, cot), dot(late, source)], axis=1)
    return out.astype(BF16).reshape(experts, 8, 2 * width + half)


def unpack_messages(recv, width):
    n = recv.shape[0]
    half = width // 2
    m8 = recv[:, :, :width].reshape(n * 8, width)
    d8 = recv[:, :, width : 2 * width].reshape(n * 8, width)
    rest = recv[:, :, 2 * width :].reshape(n, 4, 2, half)
    m2 = jnp.concatenate([rest[:, 0], rest[:, 2]], axis=-1).reshape(n * 2, width)
    d2 = jnp.concatenate([rest[:, 1], rest[:, 3]], axis=-1).reshape(n * 2, width)
    return jnp.concatenate([m8, m2], axis=0), jnp.concatenate([d8, d2], axis=0)


def expert_pass(rows_m, rows_d, column, w_first, w_second):
    col = column.astype(F32)
    gate = jax.nn.sigmoid(jnp.sum(rows_m.astype(F32) * col[None, :], axis=1, keepdims=True))
    grad_y = (gate * rows_d.astype(F32)).astype(BF16)
    rows = 0.0
    dgate = 0.0
    firsts, seconds = [], []
    for i in range(w_first.shape[0]):
        pre = dot(rows_m, w_first[i])
        value, slope = gelu_parts(pre)
        hidden = value.astype(BF16)
        back = dot_nt(rows_d, w_second[i])
        dgate = dgate + jnp.sum(hidden.astype(F32) * back, axis=1, keepdims=True)
        grad_pre = (gate * back * slope).astype(BF16)
        seconds.append(dot_tn(hidden, grad_y).astype(BF16))
        firsts.append(dot_tn(rows_m, grad_pre).astype(BF16))
        rows = rows + dot_nt(grad_pre, w_first[i])
    coef = dgate * gate * (1.0 - gate)
    rows = rows + coef * col[None, :]
    wide = rows_m.astype(F32)
    sums = jnp.stack([jnp.sum(wide * coef, axis=0), jnp.sum(wide * rows, axis=0)])
    return rows.astype(BF16), sums, jnp.stack(firsts), jnp.stack(seconds)


def body(prenorm_input, gain, router, routes, w_in, w_out, cotangent):
    halves = lax.axis_size("expert")
    experts = halves // 2
    tok, width = prenorm_input.shape
    all_first = lax.all_gather(w_in[0], "dp", axis=0)
    all_second = lax.all_gather(w_out[0], "dp", axis=0)
    xhat, inv, mixed = norm_pieces(prenorm_input, gain)
    ids = slot_ids(routes, experts)
    send = pack_messages(ids, mixed, cotangent, experts)
    send = jnp.repeat(send, 2, axis=0)
    recv = lax.all_to_all(send, "expert", split_axis=0, concat_axis=0, tiled=True)
    rows_m, rows_d = unpack_messages(recv, width)
    own = lax.axis_index("expert") // 2
    column = lax.dynamic_slice_in_dim(router, own, 1, 1)[:, 0]
    rows, sums, firsts, seconds = expert_pass(rows_m, rows_d, column, all_first, all_second)
    grad_in = lax.psum_scatter(firsts, "dp", scatter_dimension=0, tiled=False)[None]
    grad_out = lax.psum_scatter(seconds, "dp", scatter_dimension=0, tiled=False)[None]
    back = jnp.concatenate(
        [
            rows[: halves * 8].reshape(halves, 8, width),
            rows[halves * 8 :].reshape(halves, 2, width),
            jnp.zeros((halves, 6, width), BF16),
        ],
        axis=1,
    )
    ret = lax.all_to_all(back, "expert", split_axis=0, concat_axis=0, tiled=True)
    every = lax.all_gather(sums, ("expert", "dp"), axis=0)
    every = jnp.sum(every.reshape(experts, -1, 2, width), axis=1)
    grad_router = every[:, 0].T
    grad_gain = jnp.sum(every[:, 1], axis=0) / gain
    place = jnp.arange(halves * 16, dtype=jnp.int32)
    place = (place // 32) * 16 + place % 16
    pick = ((ids[:, :1] == place[None, :]) | (ids[:, 1:] == place[None, :])).astype(BF16)
    grad_mixed = dot(pick, ret.reshape(halves * 16, width))
    u = grad_mixed * gain[None, :]
    first = jnp.mean(u, axis=1, keepdims=True)
    second = jnp.mean(u * xhat, axis=1, keepdims=True)
    input_grad = (cotangent.astype(F32) + inv * (u - first - xhat * second)).astype(BF16)
    return (input_grad, grad_in, grad_out, grad_router, grad_gain)


def solution(mesh):
    in_specs = (
        P(("expert", "dp"), None),
        P(),
        P(),
        P(("expert", "dp"), None),
        P("expert", None, "dp"),
        P("expert", "dp", None),
        P(("expert", "dp"), None),
    )
    out_specs = (
        P(("expert", "dp"), None),
        P("expert", None, "dp"),
        P("expert", "dp", None),
        P(),
        P(),
    )
    return jax.shard_map(body, mesh=mesh, in_specs=in_specs, out_specs=out_specs, check_vma=False)
```

```python
import functools
import math

import jax
import jax.numpy as jnp
from jax import lax
from jax.experimental import pallas as pl
from jax.experimental.pallas import tpu as pltpu
from jax.sharding import PartitionSpec as P

F32 = jnp.float32
BF16 = jnp.bfloat16


def gelu_parts(pre):
    coeff = math.sqrt(2.0 / math.pi)
    inner = coeff * (pre + 0.044715 * pre * pre * pre)
    tanh_val = jnp.tanh(inner)
    value = 0.5 * pre * (1.0 + tanh_val)
    slope = 0.5 * (1.0 + tanh_val) + 0.5 * pre * (1.0 - tanh_val * tanh_val) * coeff * (
        1.0 + 3.0 * 0.044715 * pre * pre
    )
    return (value, slope)


def dot(a, b):
    return jnp.dot(a, b, preferred_element_type=F32)


def dot_nt(a, b):
    return lax.dot_general(a, b, (((1,), (1,)), ((), ())), preferred_element_type=F32)


def dot_tn(a, b):
    return lax.dot_general(a, b, (((0,), (0,)), ((), ())), preferred_element_type=F32)


def norm_pieces(block, gain):
    values = block.astype(F32)
    centred = values - jnp.mean(values, axis=1, keepdims=True)
    inv = lax.rsqrt(jnp.mean(centred * centred, axis=1, keepdims=True) + 1e-06)
    xhat = centred * inv
    return xhat, inv, (xhat * gain[None, :]).astype(BF16)


def slot_ids(routes, experts):
    tok = routes.shape[0]
    eye = jnp.arange(experts, dtype=jnp.int32)
    hot = (routes[:, :, None] == eye).astype(F32)
    named = jnp.sum(hot, axis=1).astype(BF16)
    lower = (jnp.arange(tok)[:, None] > jnp.arange(tok)[None, :]).astype(BF16)
    before = dot(lower, named)
    slot = jnp.sum(before[:, None, :] * hot, axis=2).astype(jnp.int32)
    return routes * 16 + slot


def pack_messages(ids, mixed, cot, experts):
    width = mixed.shape[1]
    half = width // 2
    row = jnp.arange(experts * 8, dtype=jnp.int32)
    main = (row // 8) * 16 + row % 8
    rest = (row // 8) * 16 + 8 + row % 2
    part = (row % 8) // 2
    first, second = ids[:, 0][None, :], ids[:, 1][None, :]
    place = ((main[:, None] == first) | (main[:, None] == second)).astype(BF16)
    late = (rest[:, None] == first) | (rest[:, None] == second)
    late = jnp.concatenate([late & (part == i)[:, None] for i in range(4)], axis=1).astype(BF16)
    source = jnp.concatenate([mixed[:, :half], cot[:, :half], mixed[:, half:], cot[:, half:]], axis=0)
    out = jnp.concatenate([dot(place, mixed), dot(place, cot), dot(late, source)], axis=1)
    return out.astype(BF16).reshape(experts, 8, 2 * width + half)


def unpack_messages(recv, width):
    n = recv.shape[0]
    half = width // 2
    m8 = recv[:, :, :width].reshape(n * 8, width)
    d8 = recv[:, :, width : 2 * width].reshape(n * 8, width)
    rest = recv[:, :, 2 * width :].reshape(n, 4, 2, half)
    m2 = jnp.concatenate([rest[:, 0], rest[:, 2]], axis=-1).reshape(n * 2, width)
    d2 = jnp.concatenate([rest[:, 1], rest[:, 3]], axis=-1).reshape(n * 2, width)
    return jnp.concatenate([m8, m2], axis=0), jnp.concatenate([d8, d2], axis=0)


def expert_pass(rows_m, rows_d, column, blocks):
    col = column.astype(F32)
    gate = jax.nn.sigmoid(jnp.sum(rows_m.astype(F32) * col[None, :], axis=1, keepdims=True))
    grad_y = (gate * rows_d.astype(F32)).astype(BF16)
    rows = 0.0
    dgate = 0.0
    firsts, seconds = [], []
    for w_first, w_second in blocks:
        pre = dot_nt(rows_m, w_first)
        value, slope = gelu_parts(pre)
        hidden = value.astype(BF16)
        back = dot_nt(rows_d, w_second)
        dgate = dgate + jnp.sum(hidden.astype(F32) * back, axis=1, keepdims=True)
        grad_pre = (gate * back * slope).astype(BF16)
        seconds.append(dot_tn(hidden, grad_y).astype(BF16))
        firsts.append(dot_tn(grad_pre, rows_m).astype(BF16))
        rows = rows + dot(grad_pre, w_first)
    coef = dgate * gate * (1.0 - gate)
    rows = rows + coef * col[None, :]
    wide = rows_m.astype(F32)
    sums = jnp.stack([jnp.sum(wide * coef, axis=0), jnp.sum(wide * rows, axis=0)])
    return rows.astype(BF16), sums, firsts, seconds


MESH_ID = pl.DeviceIdType.MESH


def dispatch_kernel(chips, groups, send_ref, w_ref, recv_ref, wall_ref, stage, a_send, a_recv, f_send, f_recv, w_send, w_recv, l_sem):
    me = lax.axis_index("expert")
    x = lax.axis_index("dp")
    chip, core = lax.div(me, 2), lax.rem(me, 2)
    sibling = me + 1 - 2 * core
    up, down = lax.rem(x + 1, groups), lax.rem(x + groups - 1, groups)
    barrier = pltpu.get_barrier_semaphore()

    def offset(i):
        return chips // 2 + lax.div(i + 1, 2) * (1 - 2 * lax.rem(i, 2))

    def greet(i, _):
        p = lax.rem(chip + offset(i), chips)
        pl.semaphore_signal(barrier, inc=1, device_id=(2 * p + core, x), device_id_type=MESH_ID)
        return 0

    lax.fori_loop(0, chips - 1, greet, 0)
    for peer in ((sibling, x), (me, up), (me, down)):
        pl.semaphore_signal(barrier, inc=1, device_id=peer, device_id_type=MESH_ID)
    pl.semaphore_wait(barrier, chips + 2)

    def remote(src, dst, s, r, peer):
        return pltpu.make_async_remote_copy(
            src_ref=src, dst_ref=dst, send_sem=s, recv_sem=r, device_id=peer, device_id_type=MESH_ID
        )

    def weight(src, slot, part, peer):
        k = 2 * slot + part
        return remote(src, wall_ref.at[slot, part], w_send.at[k], w_recv.at[k], peer)

    first_in = weight(w_ref.at[0], 0, 0, (me, up))
    first_out = weight(w_ref.at[1], 2, 1, (me, down))
    second_out = weight(w_ref.at[1], 0, 1, (me, up))
    second_in = weight(w_ref.at[0], 2, 0, (me, down))
    first_in.start()
    first_out.start()

    def push(i, _):
        p = lax.rem(chip + offset(i), chips)
        remote(send_ref.at[p], recv_ref.at[me], a_send.at[i], a_recv.at[i], (2 * p + core, x)).start()
        return 0

    lax.fori_loop(0, chips - 1, push, 0)
    second_out.start()
    second_in.start()
    mine = remote(send_ref.at[chip], recv_ref.at[me], f_send.at[chips - 1], f_recv.at[chips - 1], (sibling, x))
    mine.start()
    load = pltpu.make_async_copy(send_ref.at[chip], stage, l_sem.at[0])
    load.start()
    load.wait()
    keep = pltpu.make_async_copy(stage, recv_ref.at[me], l_sem.at[1])
    keep.start()

    def relay(i, _):
        q = 2 * lax.rem(chip - offset(i) + chips, chips) + core
        remote(send_ref.at[0], recv_ref.at[q], a_send.at[i], a_recv.at[i], (sibling, x)).wait_recv()
        remote(recv_ref.at[q], recv_ref.at[q], f_send.at[i], f_recv.at[i], (sibling, x)).start()
        return 0

    lax.fori_loop(0, chips // 2, relay, 0)
    first_in.wait_recv()
    third_in = weight(wall_ref.at[0, 0], 1, 0, (me, up))
    third_in.start()
    first_out.wait_recv()
    third_out = weight(wall_ref.at[2, 1], 1, 1, (me, down))
    third_out.start()
    lax.fori_loop(chips // 2, chips - 1, relay, 0)

    def finish(i, _):
        q = 2 * lax.rem(chip - offset(i) + chips, chips) + 1 - core
        remote(send_ref.at[0], recv_ref.at[0], a_send.at[i], a_recv.at[i], (sibling, x)).wait_send()
        fwd = remote(recv_ref.at[q], recv_ref.at[q], f_send.at[i], f_recv.at[i], (sibling, x))
        fwd.wait_send()
        fwd.wait_recv()
        return 0

    lax.fori_loop(0, chips - 1, finish, 0)
    mine.wait_send()
    remote(send_ref.at[0], recv_ref.at[sibling], f_send.at[chips - 1], f_recv.at[chips - 1], (sibling, x)).wait_recv()
    keep.wait()
    second_out.wait_recv()
    second_in.wait_recv()
    third_in.wait_recv()
    third_out.wait_recv()
    for copy in (first_in, first_out, second_out, second_in, third_in, third_out):
        copy.wait_send()


def dispatch(send, weights, groups):
    chips = send.shape[0]
    return pl.pallas_call(
        functools.partial(dispatch_kernel, chips, groups),
        out_shape=(
            jax.ShapeDtypeStruct((2 * chips,) + send.shape[1:], send.dtype),
            jax.ShapeDtypeStruct((groups - 1,) + weights.shape, weights.dtype),
        ),
        in_specs=[pl.BlockSpec(memory_space=pl.ANY)] * 2,
        out_specs=(pl.BlockSpec(memory_space=pl.ANY),) * 2,
        scratch_shapes=[
            pltpu.VMEM(send.shape[1:], send.dtype),
            pltpu.SemaphoreType.DMA((chips,)),
            pltpu.SemaphoreType.DMA((chips,)),
            pltpu.SemaphoreType.DMA((chips,)),
            pltpu.SemaphoreType.DMA((chips,)),
            pltpu.SemaphoreType.DMA((6,)),
            pltpu.SemaphoreType.DMA((6,)),
            pltpu.SemaphoreType.DMA((2,)),
        ],
        compiler_params=pltpu.CompilerParams(collective_id=0, has_side_effects=True),
        name="dispatch",
    )(send, weights)


def body(prenorm_input, gain, router, routes, w_in, w_out, cotangent):
    halves = lax.axis_size("expert")
    experts = halves // 2
    tok, width = prenorm_input.shape
    groups = lax.axis_size("dp")
    weights = jnp.stack([w_in[0].T, w_out[0]])
    xhat, inv, mixed = norm_pieces(prenorm_input, gain)
    ids = slot_ids(routes, experts)
    send = pack_messages(ids, mixed, cotangent, experts)
    recv, others = dispatch(send, weights, groups)
    rows_m, rows_d = unpack_messages(recv, width)
    own = lax.axis_index("expert") // 2
    column = lax.dynamic_slice_in_dim(router, own, 1, 1)[:, 0]
    blocks = [(weights[0], weights[1])] + [(others[j, 0], others[j, 1]) for j in range(groups - 1)]
    rows, sums, firsts, seconds = expert_pass(rows_m, rows_d, column, blocks)
    here = lax.axis_index("dp")
    order = lax.rem(here + groups - jnp.arange(groups), groups)
    firsts = jnp.take(jnp.stack(firsts), order, axis=0)
    seconds = jnp.take(jnp.stack(seconds), order, axis=0)
    grad_in = lax.psum_scatter(firsts, "dp", scatter_dimension=0, tiled=False).T[None]
    grad_out = lax.psum_scatter(seconds, "dp", scatter_dimension=0, tiled=False)[None]
    back = jnp.concatenate(
        [
            rows[: halves * 8].reshape(halves, 8, width),
            rows[halves * 8 :].reshape(halves, 2, width),
            jnp.zeros((halves, 6, width), BF16),
        ],
        axis=1,
    )
    ret = lax.all_to_all(back, "expert", split_axis=0, concat_axis=0, tiled=True)
    every = lax.all_gather(sums, ("expert", "dp"), axis=0)
    every = jnp.sum(every.reshape(experts, -1, 2, width), axis=1)
    grad_router = every[:, 0].T
    grad_gain = jnp.sum(every[:, 1], axis=0) / gain
    place = jnp.arange(halves * 16, dtype=jnp.int32)
    place = (place // 32) * 16 + place % 16
    pick = ((ids[:, :1] == place[None, :]) | (ids[:, 1:] == place[None, :])).astype(BF16)
    grad_mixed = dot(pick, ret.reshape(halves * 16, width))
    u = grad_mixed * gain[None, :]
    first = jnp.mean(u, axis=1, keepdims=True)
    second = jnp.mean(u * xhat, axis=1, keepdims=True)
    input_grad = (cotangent.astype(F32) + inv * (u - first - xhat * second)).astype(BF16)
    return (input_grad, grad_in, grad_out, grad_router, grad_gain)


def solution(mesh):
    in_specs = (
        P(("expert", "dp"), None),
        P(),
        P(),
        P(("expert", "dp"), None),
        P("expert", None, "dp"),
        P("expert", "dp", None),
        P(("expert", "dp"), None),
    )
    out_specs = (
        P(("expert", "dp"), None),
        P("expert", None, "dp"),
        P("expert", "dp", None),
        P(),
        P(),
    )
    return jax.shard_map(body, mesh=mesh, in_specs=in_specs, out_specs=out_specs, check_vma=False)
```

```python
import functools
import math

import jax
import jax.numpy as jnp
from jax import lax
from jax.experimental import pallas as pl
from jax.experimental.pallas import tpu as pltpu
from jax.sharding import PartitionSpec as P

F32 = jnp.float32
BF16 = jnp.bfloat16


def gelu_parts(pre):
    coeff = math.sqrt(2.0 / math.pi)
    inner = coeff * (pre + 0.044715 * pre * pre * pre)
    tanh_val = jnp.tanh(inner)
    value = 0.5 * pre * (1.0 + tanh_val)
    slope = 0.5 * (1.0 + tanh_val) + 0.5 * pre * (1.0 - tanh_val * tanh_val) * coeff * (
        1.0 + 3.0 * 0.044715 * pre * pre
    )
    return (value, slope)


def dot(a, b):
    return jnp.dot(a, b, preferred_element_type=F32)


def dot_nt(a, b):
    return lax.dot_general(a, b, (((1,), (1,)), ((), ())), preferred_element_type=F32)


def dot_tn(a, b):
    return lax.dot_general(a, b, (((0,), (0,)), ((), ())), preferred_element_type=F32)


def norm_pieces(block, gain):
    values = block.astype(F32)
    centred = values - jnp.mean(values, axis=1, keepdims=True)
    inv = lax.rsqrt(jnp.mean(centred * centred, axis=1, keepdims=True) + 1e-06)
    xhat = centred * inv
    return xhat, inv, (xhat * gain[None, :]).astype(BF16)


def slot_ids(routes, experts):
    tok = routes.shape[0]
    eye = jnp.arange(experts, dtype=jnp.int32)
    hot = (routes[:, :, None] == eye).astype(F32)
    named = jnp.sum(hot, axis=1).astype(BF16)
    lower = (jnp.arange(tok)[:, None] > jnp.arange(tok)[None, :]).astype(BF16)
    before = dot(lower, named)
    slot = jnp.sum(before[:, None, :] * hot, axis=2).astype(jnp.int32)
    return routes * 16 + slot


def pack_messages(ids, mixed, cot, experts):
    width = mixed.shape[1]
    half = width // 2
    row = jnp.arange(experts * 8, dtype=jnp.int32)
    main = (row // 8) * 16 + row % 8
    rest = (row // 8) * 16 + 8 + row % 2
    part = (row % 8) // 2
    first, second = ids[:, 0][None, :], ids[:, 1][None, :]
    place = ((main[:, None] == first) | (main[:, None] == second)).astype(BF16)
    late = (rest[:, None] == first) | (rest[:, None] == second)
    late = jnp.concatenate([late & (part == i)[:, None] for i in range(4)], axis=1).astype(BF16)
    source = jnp.concatenate([mixed[:, :half], cot[:, :half], mixed[:, half:], cot[:, half:]], axis=0)
    out = jnp.concatenate([dot(place, mixed), dot(place, cot), dot(late, source)], axis=1)
    return out.astype(BF16).reshape(experts, 8, 2 * width + half)


def unpack_messages(recv, width):
    n = recv.shape[0]
    half = width // 2
    m8 = recv[:, :, :width].reshape(n * 8, width)
    d8 = recv[:, :, width : 2 * width].reshape(n * 8, width)
    rest = recv[:, :, 2 * width :].reshape(n, 4, 2, half)
    m2 = jnp.concatenate([rest[:, 0], rest[:, 2]], axis=-1).reshape(n * 2, width)
    d2 = jnp.concatenate([rest[:, 1], rest[:, 3]], axis=-1).reshape(n * 2, width)
    return jnp.concatenate([m8, m2], axis=0), jnp.concatenate([d8, d2], axis=0)


def expert_pass(rows_m, rows_d, column, blocks):
    col = column.astype(F32)
    gate = jax.nn.sigmoid(jnp.sum(rows_m.astype(F32) * col[None, :], axis=1, keepdims=True))
    grad_y = (gate * rows_d.astype(F32)).astype(BF16)
    rows = 0.0
    dgate = 0.0
    firsts, seconds = [], []
    for w_first, w_second in blocks:
        pre = dot_nt(rows_m, w_first)
        value, slope = gelu_parts(pre)
        hidden = value.astype(BF16)
        back = dot_nt(rows_d, w_second)
        dgate = dgate + jnp.sum(hidden.astype(F32) * back, axis=1, keepdims=True)
        grad_pre = (gate * back * slope).astype(BF16)
        seconds.append(dot_tn(hidden, grad_y).astype(BF16))
        firsts.append(dot_tn(grad_pre, rows_m).astype(BF16))
        rows = rows + dot(grad_pre, w_first)
    coef = dgate * gate * (1.0 - gate)
    rows = rows + coef * col[None, :]
    wide = rows_m.astype(F32)
    sums = jnp.stack([jnp.sum(wide * coef, axis=0), jnp.sum(wide * rows, axis=0)])
    return rows.astype(BF16), sums, firsts, seconds


MESH_ID = pl.DeviceIdType.MESH


def dispatch_kernel(chips, groups, send_ref, w_ref, recv_ref, wall_ref, stage, a_send, a_recv, f_send, f_recv, w_send, w_recv, l_sem):
    me = lax.axis_index("expert")
    x = lax.axis_index("dp")
    chip, core = lax.div(me, 2), lax.rem(me, 2)
    sibling = me + 1 - 2 * core
    up, down = lax.rem(x + 1, groups), lax.rem(x + groups - 1, groups)
    barrier = pltpu.get_barrier_semaphore()

    def offset(i):
        return chips // 2 + lax.div(i + 1, 2) * (1 - 2 * lax.rem(i, 2))

    def greet(i, _):
        p = lax.rem(chip + offset(i), chips)
        pl.semaphore_signal(barrier, inc=1, device_id=(2 * p + core, x), device_id_type=MESH_ID)
        return 0

    lax.fori_loop(0, chips - 1, greet, 0)
    for peer in ((sibling, x), (me, up), (me, down)):
        pl.semaphore_signal(barrier, inc=1, device_id=peer, device_id_type=MESH_ID)
    pl.semaphore_wait(barrier, chips + 2)

    def remote(src, dst, s, r, peer):
        return pltpu.make_async_remote_copy(
            src_ref=src, dst_ref=dst, send_sem=s, recv_sem=r, device_id=peer, device_id_type=MESH_ID
        )

    def weight(src, slot, part, peer):
        k = 2 * slot + part
        return remote(src, wall_ref.at[slot, part], w_send.at[k], w_recv.at[k], peer)

    first_in = weight(w_ref.at[0], 0, 0, (me, up))
    first_out = weight(w_ref.at[1], 2, 1, (me, down))
    second_out = weight(w_ref.at[1], 0, 1, (me, up))
    second_in = weight(w_ref.at[0], 2, 0, (me, down))
    first_in.start()
    first_out.start()

    def push(i, _):
        p = lax.rem(chip + offset(i), chips)
        remote(send_ref.at[p], recv_ref.at[me], a_send.at[i], a_recv.at[i], (2 * p + core, x)).start()
        return 0

    lax.fori_loop(0, chips - 1, push, 0)
    second_out.start()
    second_in.start()
    mine = remote(send_ref.at[chip], recv_ref.at[me], f_send.at[chips - 1], f_recv.at[chips - 1], (sibling, x))
    mine.start()
    load = pltpu.make_async_copy(send_ref.at[chip], stage, l_sem.at[0])
    load.start()
    load.wait()
    keep = pltpu.make_async_copy(stage, recv_ref.at[me], l_sem.at[1])
    keep.start()

    def relay(i, _):
        q = 2 * lax.rem(chip - offset(i) + chips, chips) + core
        remote(send_ref.at[0], recv_ref.at[q], a_send.at[i], a_recv.at[i], (sibling, x)).wait_recv()
        remote(recv_ref.at[q], recv_ref.at[q], f_send.at[i], f_recv.at[i], (sibling, x)).start()
        return 0

    lax.fori_loop(0, chips // 2, relay, 0)
    first_in.wait_recv()
    third_in = weight(wall_ref.at[0, 0], 1, 0, (me, up))
    third_in.start()
    first_out.wait_recv()
    third_out = weight(wall_ref.at[2, 1], 1, 1, (me, down))
    third_out.start()
    lax.fori_loop(chips // 2, chips - 1, relay, 0)

    def finish(i, _):
        q = 2 * lax.rem(chip - offset(i) + chips, chips) + 1 - core
        remote(send_ref.at[0], recv_ref.at[0], a_send.at[i], a_recv.at[i], (sibling, x)).wait_send()
        fwd = remote(recv_ref.at[q], recv_ref.at[q], f_send.at[i], f_recv.at[i], (sibling, x))
        fwd.wait_send()
        fwd.wait_recv()
        return 0

    lax.fori_loop(0, chips - 1, finish, 0)
    mine.wait_send()
    remote(send_ref.at[0], recv_ref.at[sibling], f_send.at[chips - 1], f_recv.at[chips - 1], (sibling, x)).wait_recv()
    keep.wait()
    second_out.wait_recv()
    second_in.wait_recv()
    third_in.wait_recv()
    third_out.wait_recv()
    for copy in (first_in, first_out, second_out, second_in, third_in, third_out):
        copy.wait_send()


def dispatch(send, weights, groups):
    chips = send.shape[0]
    return pl.pallas_call(
        functools.partial(dispatch_kernel, chips, groups),
        out_shape=(
            jax.ShapeDtypeStruct((2 * chips,) + send.shape[1:], send.dtype),
            jax.ShapeDtypeStruct((groups - 1,) + weights.shape, weights.dtype),
        ),
        in_specs=[pl.BlockSpec(memory_space=pl.ANY)] * 2,
        out_specs=(pl.BlockSpec(memory_space=pl.ANY),) * 2,
        scratch_shapes=[
            pltpu.VMEM(send.shape[1:], send.dtype),
            pltpu.SemaphoreType.DMA((chips,)),
            pltpu.SemaphoreType.DMA((chips,)),
            pltpu.SemaphoreType.DMA((chips,)),
            pltpu.SemaphoreType.DMA((chips,)),
            pltpu.SemaphoreType.DMA((6,)),
            pltpu.SemaphoreType.DMA((6,)),
            pltpu.SemaphoreType.DMA((2,)),
        ],
        compiler_params=pltpu.CompilerParams(collective_id=0, has_side_effects=True),
        name="dispatch",
    )(send, weights)


def collect_kernel(chips, groups, back_ref, sums_ref, ret_ref, mine, other, total, extra, gsum, o_send, o_recv, s_send, s_recv, r_send, r_recv, l_sem, k_sem):
    me = lax.axis_index("expert")
    x = lax.axis_index("dp")
    chip, core = lax.div(me, 2), lax.rem(me, 2)
    sibling = me + 1 - 2 * core
    team = 2 * groups
    seat = 2 * x + core
    barrier = pltpu.get_barrier_semaphore()

    def offset(i):
        return chips // 2 + lax.div(i + 1, 2) * (1 - 2 * lax.rem(i, 2))

    def mate(d):
        k = lax.rem(seat + d, team)
        return (2 * chip + lax.rem(k, 2), lax.div(k, 2))

    def greet(i, _):
        p = lax.rem(chip + offset(i), chips)
        pl.semaphore_signal(barrier, inc=1, device_id=(2 * p + core, x), device_id_type=MESH_ID)
        return 0

    lax.fori_loop(0, chips - 1, greet, 0)
    for d in range(1, team):
        pl.semaphore_signal(barrier, inc=1, device_id=mate(d), device_id_type=MESH_ID)
    pl.semaphore_wait(barrier, chips + team - 2)

    def remote(src, dst, s, r, peer):
        return pltpu.make_async_remote_copy(
            src_ref=src, dst_ref=dst, send_sem=s, recv_sem=r, device_id=peer, device_id_type=MESH_ID
        )

    def share(d, slot):
        return remote(sums_ref, gsum.at[slot], s_send.at[d], s_recv.at[d], mate(d))

    def swap(i):
        p = lax.rem(chip + offset(i), chips)
        return remote(back_ref.at[p, 1 - core], other.at[i], o_send.at[i], o_recv.at[i], (sibling, x))

    def load(i):
        p = lax.rem(chip + offset(i), chips)
        return pltpu.make_async_copy(back_ref.at[p, core], mine.at[i], l_sem.at[i])

    for d in range(1, team):
        share(d, seat).start()
    own_sums = pltpu.make_async_copy(sums_ref, gsum.at[seat], k_sem.at[0])
    own_sums.start()

    def fetch(i, _):
        swap(i).start()
        load(i).start()
        return 0

    lax.fori_loop(0, chips, fetch, 0)
    own_sums.wait()
    for d in range(1, team):
        share(d, lax.rem(seat + team - d, team)).wait_recv()
    whole = gsum[0]
    for j in range(1, team):
        whole = whole + gsum[j]
    row = lax.broadcasted_iota(jnp.int32, extra.shape, 0)
    placed = jnp.zeros(extra.shape, F32)
    for part in range(3):
        piece = whole.astype(BF16).astype(F32)
        whole = whole - piece
        for j in range(2):
            placed = placed + jnp.where(row == 10 + 2 * part + j, piece[j : j + 1], 0.0)
    extra[...] = placed

    def add(i):
        load(i).wait()
        swap(i).wait_recv()
        total[i] = (mine[i].astype(F32) + other[i].astype(F32) + extra[...]).astype(BF16)

    def give(i, slot):
        p = lax.rem(chip + offset(i), chips)
        return remote(total.at[i], ret_ref.at[slot], r_send.at[i], r_recv.at[i], (2 * p + core, x))

    add(0)

    def step(i, _):
        add(i)
        give(i - 1, chip).start()
        return 0

    lax.fori_loop(1, chips, step, 0)
    keep = pltpu.make_async_copy(total.at[chips - 1], ret_ref.at[chip], k_sem.at[1])
    keep.start()

    def finish(i, _):
        q = lax.rem(chip - offset(i) + chips, chips)
        copy = give(i, q)
        copy.wait_send()
        copy.wait_recv()
        swap(i).wait_send()
        return 0

    lax.fori_loop(0, chips - 1, finish, 0)
    swap(chips - 1).wait_send()
    keep.wait()
    for d in range(1, team):
        share(d, seat).wait_send()


def collect(back, sums, groups):
    chips, _, slots, width = back.shape
    block = (chips, slots, width)
    return pl.pallas_call(
        functools.partial(collect_kernel, chips, groups),
        out_shape=jax.ShapeDtypeStruct(block, back.dtype),
        in_specs=[pl.BlockSpec(memory_space=pl.ANY)] * 2,
        out_specs=pl.BlockSpec(memory_space=pl.ANY),
        scratch_shapes=[
            pltpu.VMEM(block, back.dtype),
            pltpu.VMEM(block, back.dtype),
            pltpu.VMEM(block, back.dtype),
            pltpu.VMEM((slots, width), F32),
            pltpu.VMEM((2 * groups,) + sums.shape, F32),
            pltpu.SemaphoreType.DMA((chips,)),
            pltpu.SemaphoreType.DMA((chips,)),
            pltpu.SemaphoreType.DMA((2 * groups,)),
            pltpu.SemaphoreType.DMA((2 * groups,)),
            pltpu.SemaphoreType.DMA((chips,)),
            pltpu.SemaphoreType.DMA((chips,)),
            pltpu.SemaphoreType.DMA((chips,)),
            pltpu.SemaphoreType.DMA((2,)),
        ],
        compiler_params=pltpu.CompilerParams(collective_id=1, has_side_effects=True),
        name="collect",
    )(back, sums)


def body(prenorm_input, gain, router, routes, w_in, w_out, cotangent):
    halves = lax.axis_size("expert")
    experts = halves // 2
    tok, width = prenorm_input.shape
    groups = lax.axis_size("dp")
    weights = jnp.stack([w_in[0].T, w_out[0]])
    xhat, inv, mixed = norm_pieces(prenorm_input, gain)
    ids = slot_ids(routes, experts)
    send = pack_messages(ids, mixed, cotangent, experts)
    recv, others = dispatch(send, weights, groups)
    rows_m, rows_d = unpack_messages(recv, width)
    own = lax.axis_index("expert") // 2
    column = lax.dynamic_slice_in_dim(router, own, 1, 1)[:, 0]
    blocks = [(weights[0], weights[1])] + [(others[j, 0], others[j, 1]) for j in range(groups - 1)]
    rows, sums, firsts, seconds = expert_pass(rows_m, rows_d, column, blocks)
    here = lax.axis_index("dp")
    order = lax.rem(here + groups - jnp.arange(groups), groups)
    firsts = jnp.take(jnp.stack(firsts), order, axis=0)
    seconds = jnp.take(jnp.stack(seconds), order, axis=0)
    grad_in = lax.psum_scatter(firsts, "dp", scatter_dimension=0, tiled=False).T[None]
    grad_out = lax.psum_scatter(seconds, "dp", scatter_dimension=0, tiled=False)[None]
    back = jnp.concatenate(
        [
            rows[: halves * 8].reshape(halves, 8, width),
            rows[halves * 8 :].reshape(halves, 2, width),
            jnp.zeros((halves, 6, width), BF16),
        ],
        axis=1,
    )
    ret = collect(back.reshape(experts, 2, 16, width), sums, groups)
    every = ret[:, 10:12].astype(F32) + ret[:, 12:14].astype(F32) + ret[:, 14:].astype(F32)
    grad_router = every[:, 0].T
    grad_gain = jnp.sum(every[:, 1], axis=0) / gain
    place = jnp.arange(experts * 16, dtype=jnp.int32)
    pick = ((ids[:, :1] == place[None, :]) | (ids[:, 1:] == place[None, :])).astype(BF16)
    grad_mixed = dot(pick, ret.reshape(experts * 16, width))
    u = grad_mixed * gain[None, :]
    first = jnp.mean(u, axis=1, keepdims=True)
    second = jnp.mean(u * xhat, axis=1, keepdims=True)
    input_grad = (cotangent.astype(F32) + inv * (u - first - xhat * second)).astype(BF16)
    return (input_grad, grad_in, grad_out, grad_router, grad_gain)


def solution(mesh):
    in_specs = (
        P(("expert", "dp"), None),
        P(),
        P(),
        P(("expert", "dp"), None),
        P("expert", None, "dp"),
        P("expert", "dp", None),
        P(("expert", "dp"), None),
    )
    out_specs = (
        P(("expert", "dp"), None),
        P("expert", None, "dp"),
        P("expert", "dp", None),
        P(),
        P(),
    )
    return jax.shard_map(body, mesh=mesh, in_specs=in_specs, out_specs=out_specs, check_vma=False)
```

```python
import functools
import math

import jax
import jax.numpy as jnp
from jax import lax
from jax.experimental import pallas as pl
from jax.experimental.pallas import tpu as pltpu
from jax.sharding import PartitionSpec as P

F32 = jnp.float32
BF16 = jnp.bfloat16


def gelu_parts(pre):
    coeff = math.sqrt(2.0 / math.pi)
    inner = coeff * (pre + 0.044715 * pre * pre * pre)
    tanh_val = jnp.tanh(inner)
    value = 0.5 * pre * (1.0 + tanh_val)
    slope = 0.5 * (1.0 + tanh_val) + 0.5 * pre * (1.0 - tanh_val * tanh_val) * coeff * (
        1.0 + 3.0 * 0.044715 * pre * pre
    )
    return (value, slope)


def dot(a, b):
    return jnp.dot(a, b, preferred_element_type=F32)


def dot_nt(a, b):
    return lax.dot_general(a, b, (((1,), (1,)), ((), ())), preferred_element_type=F32)


def dot_tn(a, b):
    return lax.dot_general(a, b, (((0,), (0,)), ((), ())), preferred_element_type=F32)


def norm_pieces(block, gain):
    values = block.astype(F32)
    centred = values - jnp.mean(values, axis=1, keepdims=True)
    inv = lax.rsqrt(jnp.mean(centred * centred, axis=1, keepdims=True) + 1e-06)
    xhat = centred * inv
    return xhat, inv, (xhat * gain[None, :]).astype(BF16)


def slot_ids(routes, experts):
    tok = routes.shape[0]
    eye = jnp.arange(experts, dtype=jnp.int32)
    hot = (routes[:, :, None] == eye).astype(F32)
    named = jnp.sum(hot, axis=1).astype(BF16)
    lower = (jnp.arange(tok)[:, None] > jnp.arange(tok)[None, :]).astype(BF16)
    before = dot(lower, named)
    slot = jnp.sum(before[:, None, :] * hot, axis=2).astype(jnp.int32)
    return routes * 16 + slot


def pack_messages(ids, mixed, cot, experts):
    width = mixed.shape[1]
    half = width // 2
    row = jnp.arange(experts * 8, dtype=jnp.int32)
    main = (row // 8) * 16 + row % 8
    rest = (row // 8) * 16 + 8 + row % 2
    part = (row % 8) // 2
    first, second = ids[:, 0][None, :], ids[:, 1][None, :]
    place = ((main[:, None] == first) | (main[:, None] == second)).astype(BF16)
    late = (rest[:, None] == first) | (rest[:, None] == second)
    late = jnp.concatenate([late & (part == i)[:, None] for i in range(4)], axis=1).astype(BF16)
    source = jnp.concatenate([mixed[:, :half], cot[:, :half], mixed[:, half:], cot[:, half:]], axis=0)
    out = jnp.concatenate([dot(place, mixed), dot(place, cot), dot(late, source)], axis=1)
    return out.astype(BF16).reshape(experts, 8, 2 * width + half)


def unpack_messages(recv, width):
    n = recv.shape[0]
    half = width // 2
    m8 = recv[:, :, :width].reshape(n * 8, width)
    d8 = recv[:, :, width : 2 * width].reshape(n * 8, width)
    rest = recv[:, :, 2 * width :].reshape(n, 4, 2, half)
    m2 = jnp.concatenate([rest[:, 0], rest[:, 2]], axis=-1).reshape(n * 2, width)
    d2 = jnp.concatenate([rest[:, 1], rest[:, 3]], axis=-1).reshape(n * 2, width)
    return jnp.concatenate([m8, m2], axis=0), jnp.concatenate([d8, d2], axis=0)


def expert_pass(rows_m, rows_d, column, blocks):
    col = column.astype(F32)
    gate = jax.nn.sigmoid(jnp.sum(rows_m.astype(F32) * col[None, :], axis=1, keepdims=True))
    grad_y = (gate * rows_d.astype(F32)).astype(BF16)
    rows = 0.0
    dgate = 0.0
    firsts, seconds = [], []
    for w_first, w_second in blocks:
        pre = dot_nt(rows_m, w_first)
        value, slope = gelu_parts(pre)
        hidden = value.astype(BF16)
        back = dot_nt(rows_d, w_second)
        dgate = dgate + jnp.sum(hidden.astype(F32) * back, axis=1, keepdims=True)
        grad_pre = (gate * back * slope).astype(BF16)
        seconds.append(dot_tn(hidden, grad_y).astype(BF16))
        firsts.append(dot_tn(grad_pre, rows_m).astype(BF16))
        rows = rows + dot(grad_pre, w_first)
    coef = dgate * gate * (1.0 - gate)
    rows = rows + coef * col[None, :]
    wide = rows_m.astype(F32)
    sums = jnp.stack([jnp.sum(wide * coef, axis=0), jnp.sum(wide * rows, axis=0)])
    return rows.astype(BF16), sums, firsts, seconds


MESH_ID = pl.DeviceIdType.MESH


def dispatch_kernel(chips, groups, send_ref, w_ref, recv_ref, wall_ref, stage, a_send, a_recv, f_send, f_recv, w_send, w_recv, l_sem):
    me = lax.axis_index("expert")
    x = lax.axis_index("dp")
    chip, core = lax.div(me, 2), lax.rem(me, 2)
    sibling = me + 1 - 2 * core
    up, down = lax.rem(x + 1, groups), lax.rem(x + groups - 1, groups)
    barrier = pltpu.get_barrier_semaphore()

    def offset(i):
        return chips // 2 + lax.div(i + 1, 2) * (1 - 2 * lax.rem(i, 2))

    def greet(i, _):
        p = lax.rem(chip + offset(i), chips)
        pl.semaphore_signal(barrier, inc=1, device_id=(2 * p + core, x), device_id_type=MESH_ID)
        return 0

    lax.fori_loop(0, chips - 1, greet, 0)
    for peer in ((sibling, x), (me, up), (me, down)):
        pl.semaphore_signal(barrier, inc=1, device_id=peer, device_id_type=MESH_ID)
    pl.semaphore_wait(barrier, chips + 2)

    def remote(src, dst, s, r, peer):
        return pltpu.make_async_remote_copy(
            src_ref=src, dst_ref=dst, send_sem=s, recv_sem=r, device_id=peer, device_id_type=MESH_ID
        )

    def weight(src, slot, part, peer):
        k = 2 * slot + part
        return remote(src, wall_ref.at[slot, part], w_send.at[k], w_recv.at[k], peer)

    first_in = weight(w_ref.at[0], 0, 0, (me, up))
    first_out = weight(w_ref.at[1], 2, 1, (me, down))
    second_out = weight(w_ref.at[1], 0, 1, (me, up))
    second_in = weight(w_ref.at[0], 2, 0, (me, down))
    first_in.start()
    first_out.start()

    def push(i, _):
        p = lax.rem(chip + offset(i), chips)
        remote(send_ref.at[p], recv_ref.at[me], a_send.at[i], a_recv.at[i], (2 * p + core, x)).start()
        return 0

    lax.fori_loop(0, chips - 1, push, 0)
    second_out.start()
    second_in.start()
    mine = remote(send_ref.at[chip], recv_ref.at[me], f_send.at[chips - 1], f_recv.at[chips - 1], (sibling, x))
    mine.start()
    load = pltpu.make_async_copy(send_ref.at[chip], stage, l_sem.at[0])
    load.start()
    load.wait()
    keep = pltpu.make_async_copy(stage, recv_ref.at[me], l_sem.at[1])
    keep.start()

    def relay(i, _):
        q = 2 * lax.rem(chip - offset(i) + chips, chips) + core
        remote(send_ref.at[0], recv_ref.at[q], a_send.at[i], a_recv.at[i], (sibling, x)).wait_recv()
        remote(recv_ref.at[q], recv_ref.at[q], f_send.at[i], f_recv.at[i], (sibling, x)).start()
        return 0

    lax.fori_loop(0, chips // 2, relay, 0)
    first_in.wait_recv()
    third_in = weight(wall_ref.at[0, 0], 1, 0, (me, up))
    third_in.start()
    first_out.wait_recv()
    third_out = weight(wall_ref.at[2, 1], 1, 1, (me, down))
    third_out.start()
    lax.fori_loop(chips // 2, chips - 1, relay, 0)

    def finish(i, _):
        q = 2 * lax.rem(chip - offset(i) + chips, chips) + 1 - core
        remote(send_ref.at[0], recv_ref.at[0], a_send.at[i], a_recv.at[i], (sibling, x)).wait_send()
        fwd = remote(recv_ref.at[q], recv_ref.at[q], f_send.at[i], f_recv.at[i], (sibling, x))
        fwd.wait_send()
        fwd.wait_recv()
        return 0

    lax.fori_loop(0, chips - 1, finish, 0)
    mine.wait_send()
    remote(send_ref.at[0], recv_ref.at[sibling], f_send.at[chips - 1], f_recv.at[chips - 1], (sibling, x)).wait_recv()
    keep.wait()
    second_out.wait_recv()
    second_in.wait_recv()
    third_in.wait_recv()
    third_out.wait_recv()
    for copy in (first_in, first_out, second_out, second_in, third_in, third_out):
        copy.wait_send()


def dispatch(send, weights, groups):
    chips = send.shape[0]
    return pl.pallas_call(
        functools.partial(dispatch_kernel, chips, groups),
        out_shape=(
            jax.ShapeDtypeStruct((2 * chips,) + send.shape[1:], send.dtype),
            jax.ShapeDtypeStruct((groups - 1,) + weights.shape, weights.dtype),
        ),
        in_specs=[pl.BlockSpec(memory_space=pl.ANY)] * 2,
        out_specs=(pl.BlockSpec(memory_space=pl.ANY),) * 2,
        scratch_shapes=[
            pltpu.VMEM(send.shape[1:], send.dtype),
            pltpu.SemaphoreType.DMA((chips,)),
            pltpu.SemaphoreType.DMA((chips,)),
            pltpu.SemaphoreType.DMA((chips,)),
            pltpu.SemaphoreType.DMA((chips,)),
            pltpu.SemaphoreType.DMA((6,)),
            pltpu.SemaphoreType.DMA((6,)),
            pltpu.SemaphoreType.DMA((2,)),
        ],
        compiler_params=pltpu.CompilerParams(collective_id=0, has_side_effects=True),
        name="dispatch",
    )(send, weights)


def collect_kernel(chips, groups, back_ref, sums_ref, ret_ref, mine, other, total, extra, gsum, o_send, o_recv, s_send, s_recv, r_send, r_recv, l_sem, k_sem):
    me = lax.axis_index("expert")
    x = lax.axis_index("dp")
    chip, core = lax.div(me, 2), lax.rem(me, 2)
    sibling = me + 1 - 2 * core
    team = 2 * groups
    seat = 2 * x + core
    barrier = pltpu.get_barrier_semaphore()

    def offset(i):
        return chips // 2 + lax.div(i + 1, 2) * (1 - 2 * lax.rem(i, 2))

    def mate(d):
        k = lax.rem(seat + d, team)
        return (2 * chip + lax.rem(k, 2), lax.div(k, 2))

    def greet(i, _):
        p = lax.rem(chip + offset(i), chips)
        pl.semaphore_signal(barrier, inc=1, device_id=(2 * p + core, x), device_id_type=MESH_ID)
        return 0

    lax.fori_loop(0, chips - 1, greet, 0)
    for d in range(1, team):
        pl.semaphore_signal(barrier, inc=1, device_id=mate(d), device_id_type=MESH_ID)
    pl.semaphore_wait(barrier, chips + team - 2)

    def remote(src, dst, s, r, peer):
        return pltpu.make_async_remote_copy(
            src_ref=src, dst_ref=dst, send_sem=s, recv_sem=r, device_id=peer, device_id_type=MESH_ID
        )

    def share(d, slot):
        return remote(sums_ref, gsum.at[slot], s_send.at[d], s_recv.at[d], mate(d))

    def swap(i):
        p = lax.rem(chip + offset(i), chips)
        return remote(back_ref.at[p, 1 - core], other.at[i], o_send.at[i], o_recv.at[i], (sibling, x))

    def load(i):
        p = lax.rem(chip + offset(i), chips)
        return pltpu.make_async_copy(back_ref.at[p, core], mine.at[i], l_sem.at[i])

    for d in range(1, team):
        share(d, seat).start()
    own_sums = pltpu.make_async_copy(sums_ref, gsum.at[seat], k_sem.at[0])
    own_sums.start()

    def fetch(i, _):
        swap(i).start()
        load(i).start()
        return 0

    lax.fori_loop(0, chips, fetch, 0)
    own_sums.wait()
    for d in range(1, team):
        share(d, lax.rem(seat + team - d, team)).wait_recv()
    whole = gsum[0]
    for j in range(1, team):
        whole = whole + gsum[j]
    row = lax.broadcasted_iota(jnp.int32, extra.shape, 0)
    placed = jnp.zeros(extra.shape, F32)
    for part in range(3):
        piece = whole.astype(BF16).astype(F32)
        whole = whole - piece
        for j in range(2):
            placed = placed + jnp.where(row == 10 + 2 * part + j, piece[j : j + 1], 0.0)
    extra[...] = placed

    def add(i):
        load(i).wait()
        swap(i).wait_recv()
        total[i] = (mine[i].astype(F32) + other[i].astype(F32) + extra[...]).astype(BF16)

    def give(i, slot):
        p = lax.rem(chip + offset(i), chips)
        return remote(total.at[i], ret_ref.at[slot], r_send.at[i], r_recv.at[i], (2 * p + core, x))

    add(0)

    def step(i, _):
        add(i)
        give(i - 1, chip).start()
        return 0

    lax.fori_loop(1, chips, step, 0)
    keep = pltpu.make_async_copy(total.at[chips - 1], ret_ref.at[chip], k_sem.at[1])
    keep.start()

    def finish(i, _):
        q = lax.rem(chip - offset(i) + chips, chips)
        copy = give(i, q)
        copy.wait_send()
        copy.wait_recv()
        swap(i).wait_send()
        return 0

    lax.fori_loop(0, chips - 1, finish, 0)
    swap(chips - 1).wait_send()
    keep.wait()
    for d in range(1, team):
        share(d, seat).wait_send()


def collect(back, sums, groups):
    chips, _, slots, width = back.shape
    block = (chips, slots, width)
    return pl.pallas_call(
        functools.partial(collect_kernel, chips, groups),
        out_shape=jax.ShapeDtypeStruct(block, back.dtype),
        in_specs=[pl.BlockSpec(memory_space=pl.ANY)] * 2,
        out_specs=pl.BlockSpec(memory_space=pl.ANY),
        scratch_shapes=[
            pltpu.VMEM(block, back.dtype),
            pltpu.VMEM(block, back.dtype),
            pltpu.VMEM(block, back.dtype),
            pltpu.VMEM((slots, width), F32),
            pltpu.VMEM((2 * groups,) + sums.shape, F32),
            pltpu.SemaphoreType.DMA((chips,)),
            pltpu.SemaphoreType.DMA((chips,)),
            pltpu.SemaphoreType.DMA((2 * groups,)),
            pltpu.SemaphoreType.DMA((2 * groups,)),
            pltpu.SemaphoreType.DMA((chips,)),
            pltpu.SemaphoreType.DMA((chips,)),
            pltpu.SemaphoreType.DMA((chips,)),
            pltpu.SemaphoreType.DMA((2,)),
        ],
        compiler_params=pltpu.CompilerParams(collective_id=1, has_side_effects=True),
        name="collect",
    )(back, sums)


def body(prenorm_input, gain, router, routes, w_in, w_out, cotangent):
    halves = lax.axis_size("expert")
    experts = halves // 2
    tok, width = prenorm_input.shape
    groups = lax.axis_size("dp")
    weights = jnp.stack([w_in[0].T, w_out[0]])
    xhat, inv, mixed = norm_pieces(prenorm_input, gain)
    ids = slot_ids(routes, experts)
    send = pack_messages(ids, mixed, cotangent, experts)
    recv, others = dispatch(send, weights, groups)
    rows_m, rows_d = unpack_messages(recv, width)
    own = lax.axis_index("expert") // 2
    column = lax.dynamic_slice_in_dim(router, own, 1, 1)[:, 0]
    blocks = [(weights[0], weights[1])] + [(others[j, 0], others[j, 1]) for j in range(groups - 1)]
    rows, sums, firsts, seconds = expert_pass(rows_m, rows_d, column, blocks)
    here = lax.axis_index("dp")
    order = lax.rem(here + groups - jnp.arange(groups), groups)
    firsts = jnp.take(jnp.stack(firsts), order, axis=0, mode="clip")
    seconds = jnp.take(jnp.stack(seconds), order, axis=0, mode="clip")
    grad_in = lax.psum_scatter(firsts, "dp", scatter_dimension=0, tiled=False).T[None]
    grad_out = lax.psum_scatter(seconds, "dp", scatter_dimension=0, tiled=False)[None]
    back = jnp.concatenate(
        [
            rows[: halves * 8].reshape(halves, 8, width),
            rows[halves * 8 :].reshape(halves, 2, width),
            jnp.zeros((halves, 6, width), BF16),
        ],
        axis=1,
    )
    ret = collect(back.reshape(experts, 2, 16, width), sums, groups)
    every = ret[:, 10:12].astype(F32) + ret[:, 12:14].astype(F32) + ret[:, 14:].astype(F32)
    grad_router = every[:, 0].T
    grad_gain = jnp.sum(every[:, 1], axis=0) / gain
    place = jnp.arange(experts * 16, dtype=jnp.int32)
    pick = ((ids[:, :1] == place[None, :]) | (ids[:, 1:] == place[None, :])).astype(BF16)
    grad_mixed = dot(pick, ret.reshape(experts * 16, width))
    u = grad_mixed * gain[None, :]
    first = jnp.mean(u, axis=1, keepdims=True)
    second = jnp.mean(u * xhat, axis=1, keepdims=True)
    input_grad = (cotangent.astype(F32) + inv * (u - first - xhat * second)).astype(BF16)
    return (input_grad, grad_in, grad_out, grad_router, grad_gain)


def solution(mesh):
    in_specs = (
        P(("expert", "dp"), None),
        P(),
        P(),
        P(("expert", "dp"), None),
        P("expert", None, "dp"),
        P("expert", "dp", None),
        P(("expert", "dp"), None),
    )
    out_specs = (
        P(("expert", "dp"), None),
        P("expert", None, "dp"),
        P("expert", "dp", None),
        P(),
        P(),
    )
    return jax.shard_map(body, mesh=mesh, in_specs=in_specs, out_specs=out_specs, check_vma=False)
```
